32 devices in a mesh: pipe: 2 (over core), expert: 16 (over z, y, x).
Axes of the slice: x: 2, y: 2, z: 4, core: 2. Of those that a mesh axis runs over, the one named last changes fastest.
Arguments:
- tokens: bfloat16 [2048, 3584], P('expert'), may hold values from -6 to 6
- expert_ids: int32 [2048, 8], P('expert'), may hold values from 0 to 15, all different within a row; in each aligned block of 128 rows (0 to 127, 128 to 255, ...) at most 80 rows name the same one
- combine_weights: float32 [2048, 8], P('expert'), may hold values from 0.1 to 1
- w_gate: bfloat16 [16, 3584, 2048], P('expert', None, 'pipe'), may hold values from -0.09375 to 0.09375
- w_up: bfloat16 [16, 3584, 2048], P('expert', None, 'pipe'), may hold values from -0.09375 to 0.09375
- w_down: bfloat16 [16, 2048, 3584], P('expert', None, 'pipe'), may hold values from -0.125 to 0.125
Outputs:
- mixture: bfloat16 [2048, 3584], P('expert', 'pipe')
The draws below stay inside these ranges and needn't reach their ends.
Inputs may be any that keep to these rules, and one draw needn't show every extreme that they name: `expert_ids`: each row names 8 different experts. Token t belongs to group t // 128; among the rows of one group no expert is named more than 80 times, and some group names some expert exactly 80 times.
All inputs are finite; a program needn't handle non-finite values.
Results may differ from the reference program's by a relative error of at most 0.0058.
Values may be sent and summed in bfloat16 or wider, within the bound.
A program may use at most 128 MiB of HBM per device.

```python
import math
import jax
import jax.numpy as jnp
import numpy as np
from jax import lax

D = 3584
FF = 2048
TOPK = 8
TOK_DEV = 128
EXPERTS = 16
TOKENS = 2048
CAP = 80
N_EXPERT = 16


def steps_of(key, dims, cuts, smallest, top_value):
    def one(dim, blocks):
        steps = jax.random.uniform(jax.random.fold_in(jax.random.fold_in(key, 6), dim), (blocks,), jnp.float32, smallest / len(cuts), top_value / len(cuts))
        return jnp.repeat(jnp.exp(steps), dims[dim] // blocks).reshape((-1,) + (1,) * (len(dims) - dim - 1))

    factor_of = one(*cuts[0])
    for cut in cuts[1:]:
        factor_of = factor_of * one(*cut)
    return factor_of


def routed_block(rng, own, number, rows, amount, top, most, skew):
    ranking = jax.random.permutation(rng, amount)
    crowded, common = load_shares(amount, rows * top, most, skew, True), load_shares(amount, rows * top, most, skew, False)
    places = jnp.arange(amount)

    def named(sizes, turn):
        used = int((sizes > 0).sum())
        fixed = max(1, used // 4)
        moved = fixed + (places - fixed + turn * (used - fixed)) % max(1, amount - fixed)
        return jnp.zeros((amount,), jnp.int32).at[ranking[jnp.where(places < fixed, places, moved)]].set(jnp.asarray(sizes, jnp.int32))

    sizes = jnp.where(number % 4 == 0, named(crowded, number // 4), named(common, number - number // 4 - 1))
    mixed = jax.random.permutation(jax.random.fold_in(own, 3), amount)
    donor, sink = mixed[0:amount // 2 * 2:2], mixed[1:amount // 2 * 2:2]
    room = jnp.minimum(sizes[donor] - 1, most - sizes[sink]) // 2
    room = jnp.where((donor == ranking[0]) | (sink == ranking[0]) | (sizes[sink] == 0), 0, jnp.maximum(room, 0))
    moved = jax.random.randint(jax.random.fold_in(own, 4), (amount // 2,), 0, 1 << 20) % (room + 1)
    sizes = sizes.at[donor].add(-moved).at[sink].add(moved)
    labels = jnp.searchsorted(jnp.cumsum(sizes), jnp.arange(rows * top), side="right").astype(jnp.int32)
    grid = labels.reshape(top, rows).T
    grid = grid[jax.random.permutation(jax.random.fold_in(own, 1), rows)]
    turn = jax.random.randint(jax.random.fold_in(own, 2), (rows, 1), 0, top)
    return jnp.take_along_axis(grid, (jnp.arange(top)[None, :] + turn) % top, axis=1)


def load_shares(amount, total, bound, lean, full):
    portions = [(1 << 20) // math.isqrt(grade ** lean) + 1 for grade in range(1, amount + 1)]
    largest = bound if full else min(bound, max(-(-total // amount), total * portions[0] // sum(portions)))
    least = 1 if total - largest >= amount - 1 else 0
    given, rest = [largest] + [least] * (amount - 1), total - largest - least * (amount - 1)
    while rest > 0:
        free = [i for i in range(1, amount) if given[i] < largest] or [i for i in range(1, amount) if given[i] < bound]
        mass, remaining = sum([portions[i] for i in free]), rest
        for i in free:
            extra = min(bound - given[i], max(1, remaining * portions[i] // mass), rest)
            given[i] = given[i] + extra
            rest = rest - extra
    return np.array(given)


def scatter_about(key, extent, spread, bound, shards=(), kind=jnp.bfloat16):
    values = spread * jax.random.normal(key, extent, jnp.float32)
    if shards:
        values = values * steps_of(key, extent, shards, -0.22, 0.18)
    return jnp.clip(values, -bound, bound).astype(kind)


def setup_inputs(seed: int = 0) -> dict:
    arg_keys = jax.random.split(jax.random.key(seed), 7)
    tokens = scatter_about(arg_keys[0], (TOKENS, D), 1.0, 6.0, ((0, 16),))
    expert_ids_keys = jax.random.split(jax.random.fold_in(arg_keys[1], 1), TOKENS // TOK_DEV)
    expert_ids_turns = jax.random.permutation(jax.random.fold_in(arg_keys[1], 3), TOKENS // TOK_DEV)
    expert_ids = jax.vmap(lambda own, number: routed_block(jax.random.fold_in(arg_keys[1], 2), own, number, TOK_DEV, EXPERTS, TOPK, CAP, 2))(expert_ids_keys, expert_ids_turns).reshape((TOKENS, TOPK))
    combine_weights = jnp.clip(0.1 + 0.9 * jax.random.uniform(arg_keys[2], (TOKENS, TOPK), jnp.float32) ** steps_of(arg_keys[2], (TOKENS, TOPK), ((0, 16),), -0.2, 0.2), 0.1, 1.0)
    w_gate = scatter_about(arg_keys[3], (EXPERTS, D, FF), D ** -0.5, 0.09375, ((0, 16), (2, 2)))
    w_up = scatter_about(arg_keys[4], (EXPERTS, D, FF), D ** -0.5, 0.09375, ((0, 16), (2, 2)))
    w_down = scatter_about(arg_keys[5], (EXPERTS, FF, D), FF ** -0.5, 0.125, ((0, 16), (2, 2)))
    return dict(tokens=tokens, expert_ids=expert_ids, combine_weights=combine_weights, w_gate=w_gate, w_up=w_up, w_down=w_down)


def reference(tokens, expert_ids, combine_weights, w_gate, w_up, w_down):
    group_count = N_EXPERT
    grouped_ids = expert_ids.reshape(group_count, TOK_DEV, TOPK).astype(jnp.int32)
    expert_iota = jnp.arange(EXPERTS).astype(jnp.int32)
    chosen = (grouped_ids[..., None] == expert_iota).astype(jnp.int32)
    expert_hits = jnp.sum(chosen, axis=2)
    rank_table = jnp.cumsum(expert_hits, axis=1) - expert_hits
    slot_rank = jnp.sum(chosen * rank_table[:, :, None, :], axis=3).astype(jnp.int32)
    group_index = jnp.arange(group_count).astype(jnp.int32)[:, None, None]
    column = (group_index * CAP + slot_rank).astype(jnp.int32)
    token_index = group_index * TOK_DEV + jnp.arange(TOK_DEV).astype(jnp.int32)[None, :, None]
    token_index = jnp.broadcast_to(token_index, grouped_ids.shape).astype(jnp.int32)
    token_table = jnp.full((EXPERTS, group_count * CAP), TOKENS, jnp.int32)
    token_table = token_table.at[grouped_ids, column].set(token_index)
    weight_table = jnp.zeros((EXPERTS, group_count * CAP), jnp.float32)
    weight_table = weight_table.at[grouped_ids, column].set(combine_weights.reshape(group_count, TOK_DEV, TOPK))
    padded = jnp.concatenate([tokens, jnp.zeros((1, D), tokens.dtype)], axis=0)

    def one_expert(running, expert):
        rows_here = token_table[expert]
        gathered = padded[rows_here]
        gate = jnp.dot(gathered, w_gate[expert], preferred_element_type=jnp.float32)
        up_val = jnp.dot(gathered, w_up[expert], preferred_element_type=jnp.float32)
        hidden = (jax.nn.silu(gate) * up_val).astype(jnp.bfloat16)
        expert_out = jnp.dot(hidden, w_down[expert], preferred_element_type=jnp.float32).astype(jnp.bfloat16)
        weighted = weight_table[expert][:, None] * expert_out.astype(jnp.float32)
        return running.at[rows_here].add(weighted), None

    start_acc = jnp.zeros((TOKENS + 1, D), jnp.float32)
    final_acc, unused = lax.scan(one_expert, start_acc, jnp.arange(EXPERTS).astype(jnp.int32))
    return final_acc[:TOKENS].astype(jnp.bfloat16)
```

```python
import functools
import jax
import jax.numpy as jnp
from jax import lax
from jax.experimental import pallas as pl
from jax.experimental.pallas import tpu as pltpu
from jax.sharding import PartitionSpec as P

LAYERS, SIDE = 4, 2
MESH = pl.DeviceIdType.MESH
BF16, F32 = jnp.bfloat16, jnp.float32
TILE = 256
SEMS = 176
IN, OUT = 0, 1


def moe_kernel(
    cap, tok_hbm, table_ref, wg_hbm, wu_hbm, wd_hbm, out_ref,
    full, first, leaf, rows, hidden, outs, row_weight, tabs, slots, marks,
    trim, sums_out, sums_in, zsend, zpass, zfin, wg, wu, wd,
    send_sem, recv_sem, local_sem,
):
    p = lax.axis_index("pipe")
    me = lax.axis_index("expert")
    z, y, x = me // 4, lax.rem(me // 2, 2), lax.rem(me, 2)
    toks, share = full.shape[1:]
    half = share // 2
    ff = wg.shape[1]
    base = pl.multiple_of(p * share, 128)
    mid = lax.rem((z + 1) // 2, 2)
    is_mid, is_end = mid == 1, mid == 0
    step = 1 - 2 * (z // 2)

    def chip(zz, yy, xx):
        return {"pipe": p, "expert": zz * 4 + yy * 2 + xx}

    xn, yn, dn = chip(z, y, 1 - x), chip(z, 1 - y, x), chip(z, 1 - y, 1 - x)
    inward = chip(z + step, y, x)
    outward = chip(z - step * mid, y, x)
    twin = {"pipe": 1 - p, "expert": me}
    layer = z * 4
    e_x, e_y = layer + y * 2 + 1 - x, layer + (1 - y) * 2 + x
    g_me, g_y, g_x, g_d = y * 2 + x, (1 - y) * 2 + x, y * 2 + 1 - x, (1 - y) * 2 + 1 - x

    keys = {}
    unsent = []

    def sem(*key):
        return keys.setdefault(key, len(keys))

    def make(skey, rkey, source, slot, device):
        source, slot = (ref() if callable(ref) else ref for ref in (source, slot))
        return pltpu.make_async_remote_copy(
            src_ref=source, dst_ref=slot, send_sem=send_sem.at[sem("s", *skey)],
            recv_sem=recv_sem.at[sem("s", *rkey)], device_id=device, device_id_type=MESH,
        )

    def send(skey, rkey, source, slot, device, when=None):
        make(skey, rkey, source, slot, device).start()
        unsent.append((when, functools.partial(make, skey, rkey, source, slot, device)))

    def arrived(rkey, slot):
        make(rkey, rkey, slot, slot, xn).wait_recv()

    def cols(h):
        return pl.ds(h * half, half)

    def wide_cols(h):
        return pl.ds(pl.multiple_of(base + h * half, 128), half)

    def load_tokens():
        return pltpu.make_async_copy(tok_hbm.at[:, pl.ds(base, share)], full.at[0], local_sem.at[3])

    weight_loads = [
        pltpu.make_async_copy(wg_hbm.at[0], wg, local_sem.at[0]),
        pltpu.make_async_copy(wu_hbm.at[0], wu, local_sem.at[1]),
        pltpu.make_async_copy(wd_hbm.at[0], wd, local_sem.at[2]),
    ]
    load_tokens().start()
    barrier = pltpu.get_barrier_semaphore()
    for device in (xn, yn, dn, twin, inward):
        pl.semaphore_signal(barrier, inc=1, device_id=device, device_id_type=MESH)

    @pl.when(is_mid)
    def _():
        pl.semaphore_signal(barrier, inc=1, device_id=outward, device_id_type=MESH)

    for copy in weight_loads:
        copy.start()
    tabs[0, g_me] = table_ref[...]

    def earlier():
        a = lax.broadcasted_iota(jnp.int32, (toks, toks), 0)
        return jnp.where(a < lax.broadcasted_iota(jnp.int32, (toks, toks), 1), 1.0, 0.0).astype(BF16)

    def rank(c, g):
        table = tabs[c, g]
        named = table > 0.0
        order = jnp.dot(jnp.where(named, 1.0, 0.0).astype(BF16), earlier(), preferred_element_type=F32)
        slots[c, g] = jnp.where(named, order.astype(jnp.int32), -1)

    def picks(c, g, e):
        place = slots[c, g, pl.ds(e, 1), :]
        return place == lax.broadcasted_iota(jnp.int32, (cap, toks), 0)

    def mark(c, k, g, other):
        marks[c, k, pl.ds(0, cap)] = jnp.where(picks(c, g, me), 1.0, 0.0).astype(BF16)
        marks[c, k, pl.ds(cap, cap)] = jnp.where(picks(c, g, other), 1.0, 0.0).astype(BF16)

    rank(0, g_me)
    mark(0, 0, g_me, e_x)
    mark(0, 1, g_me, e_y)
    pl.semaphore_wait(barrier, 5 + mid)
    load_tokens().wait()

    def z_hop(name, c, target, device, h, when):
        send(
            (name, h), ("zf", target, h), lambda: full.at[c, :, cols(h)],
            lambda: full.at[target, :, cols(h)], device, when,
        )
        if h == 0:
            send(
                (name, "t"), ("zf", target, "t"), lambda: tabs.at[c, g_me],
                lambda: tabs.at[target, g_me], device, when,
            )

    def start_z():
        for h in range(2):
            @pl.when(is_mid)
            def _():
                z_hop("own", 0, 1, inward, h, is_mid)
                z_hop("own_out", 0, 1, outward, h, is_mid)

            @pl.when(is_end)
            def _():
                z_hop("own_end", 0, 3, inward, h, is_end)

    def z_wait(c, h):
        arrived(("zf", c, h), full.at[c, :, cols(h)])
        if h == 0:
            arrived(("zf", c, "t"), tabs.at[c, g_me])

    def d1(c):
        for h in range(2):
            if c in (1, 2):
                z_wait(c, h)

                @pl.when(is_mid)
                def _():
                    z_hop(f"pass{c}", c, c + 1, outward, h, is_mid)
            if c == 1:
                @pl.when(is_mid)
                def _():
                    z_wait(3, h)
                    z_hop("pass3", 3, 2, inward, h, is_mid)
            if c == 3:
                @pl.when(is_end)
                def _():
                    z_wait(3, h)
            if h == 0:
                for name, device in (("y", yn), ("x", xn), ("d", dn)):
                    key = ("tab" + name, c)
                    send(key, key, tabs.at[c, g_me], tabs.at[c, g_me], device)
            key = ("first", c, h)
            send(key, key, full.at[c, :, cols(h)], first.at[c, h], xn if h else yn)

    def pack(c, k, h, g, source, device):
        packed = jnp.dot(marks[c, k], source, preferred_element_type=F32).astype(BF16)
        rows[c, g, :, wide_cols(h)] = packed[:cap]
        leaf[c, k] = packed[cap:]
        key = ("leaf", c, k)
        send(key, key, leaf.at[c, k], rows.at[c, g, :, wide_cols(h)], device)

    def d2(c):
        if c:
            rank(c, g_me)
            mark(c, 0, g_me, e_x)
            mark(c, 1, g_me, e_y)
        pack(c, 0, 0, g_me, full[c, :, cols(0)], xn)
        pack(c, 1, 1, g_me, full[c, :, cols(1)], yn)

    def d3(c):
        for name, g in (("y", g_y), ("x", g_x), ("d", g_d)):
            arrived(("tab" + name, c), tabs.at[c, g])
            rank(c, g)
        mark(c, 2, g_y, e_x)
        mark(c, 3, g_x, e_y)
        arrived(("first", c, 0), first.at[c, 0])
        pack(c, 2, 0, g_y, first[c, 0], xn)
        arrived(("first", c, 1), first.at[c, 1])
        pack(c, 3, 1, g_x, first[c, 1], yn)

    def d4(c):
        for k, g, h in ((0, g_x, 0), (1, g_y, 1), (2, g_d, 0), (3, g_d, 1)):
            arrived(("leaf", c, k), rows.at[c, g, :, wide_cols(h)])
        mine = rows.at[c, :, :, pl.ds(base, share)]
        send(("twin", c), ("twin", c), mine, mine, twin)

    def twin_hidden(c, n):
        tile = hidden.at[c, :, pl.ds(pl.multiple_of(p * ff + n * TILE, TILE), TILE)]
        at = sem("hidden", c, 0) + n
        return pltpu.make_async_remote_copy(
            src_ref=tile, dst_ref=tile, send_sem=send_sem.at[at], recv_sem=recv_sem.at[at],
            device_id=twin, device_id_type=MESH,
        )

    ff_tiles = ff // TILE

    def gate_up(c):
        for n in range(ff_tiles):
            sem("hidden", c, n)
        arrived(("twin", c), rows.at[c, :, :, pl.ds(0, share)])
        if c == 0:
            weight_loads[0].wait()
            weight_loads[1].wait()

        def tile(n, carry):
            at = pl.ds(pl.multiple_of(n * TILE, TILE), TILE)
            mine = rows[c].reshape(4 * cap, 2 * share)
            gate = jnp.dot(mine, wg[:, at], preferred_element_type=F32)
            up = jnp.dot(mine, wu[:, at], preferred_element_type=F32)
            value = (gate / (1.0 + jnp.exp(-gate)) * up).astype(BF16)
            hidden[c, :, pl.ds(pl.multiple_of(p * ff + n * TILE, TILE), TILE)] = value
            twin_hidden(c, n).start()
            return carry

        lax.fori_loop(0, ff_tiles, tile, 0)

    def down(c):
        for g in range(4):
            weight = tabs[c, g, pl.ds(me, 1), :]
            column = jnp.sum(jnp.where(picks(c, g, me), weight, 0.0), axis=1, keepdims=True)
            row_weight[pl.ds(g * cap, cap)] = jnp.broadcast_to(column, (cap, 128))
        if c == 0:
            weight_loads[2].wait()

        def landed(n, carry):
            twin_hidden(c, n).wait_recv()
            return carry

        lax.fori_loop(0, ff_tiles, landed, 0)

        def tile(n, carry):
            at = pl.ds(pl.multiple_of(n * TILE, TILE), TILE)
            value = jnp.dot(hidden[c], wd[:, at], preferred_element_type=F32)
            scale = row_weight[...]
            value = value * jnp.concatenate([scale] * (TILE // 128), axis=1)
            outs[c, :, :, at] = value.astype(BF16).reshape(4, cap, TILE)
            return carry

        lax.fori_loop(0, share // TILE, tile, 0)

    def c1(c):
        for j, h, g, device in ((1, 0, g_d, xn), (1, 1, g_d, yn), (0, 0, g_x, xn), (0, 1, g_y, yn)):
            key = ("trim", c, h, j)
            send(key, key, outs.at[c, g, :, cols(h)], trim.at[c, h, j], device)

    def spread(c, k, g, h, j):
        arrived(("trim", c, h, j), trim.at[c, h, j])
        dims = (((0,), (0,)), ((), ()))
        one = lax.dot_general(marks[c, k, pl.ds(0, cap)], outs[c, g, :, cols(h)], dims, preferred_element_type=F32)
        return one + lax.dot_general(marks[c, k, pl.ds(cap, cap)], trim[c, h, j], dims, preferred_element_type=F32)

    def c2(c):
        for h, k, g, device in ((0, 2, g_y, yn), (1, 3, g_x, xn)):
            sums_out[c, h] = spread(c, k, g, h, 1).astype(BF16)
            key = ("sums", c, h)
            send(key, key, sums_out.at[c, h], sums_in.at[c, h], device)

    def layer_sum(c, h):
        value = spread(c, h, g_me, h, 0)
        arrived(("sums", c, h), sums_in.at[c, h])
        return value + sums_in[c, h].astype(F32)

    def z_sum(name, c, h, target, device, when):
        buffer, at = target
        send(
            (name, c, h), ("zpass" if buffer is zpass else "zfin", at, h),
            lambda: zsend.at[c - 1, :, cols(h)], lambda: buffer.at[at, :, cols(h)], device, when,
        )

    def c3(c):
        for h in range(2):
            zsend[c - 1, :, cols(h)] = layer_sum(c, h).astype(BF16)

            @pl.when(is_end)
            def _():
                z_sum("zend", c, h, (zfin, OUT) if c == 1 else (zpass, c - 2), inward, is_end)

    def z_mid(c):
        @pl.when(is_mid)
        def _():
            for h in range(2):
                arrived(("zpass", c - 1, h), zpass.at[c - 1, :, cols(h)])
                total = zsend[c - 1, :, cols(h)].astype(F32) + zpass[c - 1, :, cols(h)].astype(F32)
                zsend[c - 1, :, cols(h)] = total.astype(BF16)
                z_sum("zmid", c, h, (zpass, 2) if c == 2 else (zfin, IN), outward if c == 3 else inward, is_mid)

    start_z()
    d1(0)
    d2(0)
    d3(0)
    d1(1)
    d2(1)
    d4(0)
    gate_up(0)
    d3(1)
    d1(2)
    d2(2)
    d4(1)
    down(0)
    gate_up(1)
    d3(2)
    d1(3)
    d2(3)
    d4(2)
    down(1)
    gate_up(2)
    d3(3)
    c1(1)
    d4(3)
    down(2)
    c1(2)
    c2(1)
    gate_up(3)
    c3(1)
    down(3)
    c1(3)
    c2(2)
    c1(0)
    c3(2)
    c2(3)
    z_mid(1)
    c3(3)
    c2(0)
    z_mid(2)
    own = [layer_sum(0, h) for h in range(2)]
    z_mid(3)
    for h in range(2):
        arrived(("zfin", IN, h), zfin.at[IN, :, cols(h)])

        @pl.when(is_mid)
        def _():
            arrived(("zfin", OUT, h), zfin.at[OUT, :, cols(h)])
            value = own[h] + zfin[IN, :, cols(h)].astype(F32) + zfin[OUT, :, cols(h)].astype(F32)
            out_ref[:, cols(h)] = value.astype(BF16)

        @pl.when(is_end)
        def _():
            out_ref[:, cols(h)] = (own[h] + zfin[IN, :, cols(h)].astype(F32)).astype(BF16)

    for c in range(4):
        lax.fori_loop(0, ff_tiles, lambda n, carry, c=c: (twin_hidden(c, n).wait_send(), carry)[1], 0)
    for cond in (None, is_mid, is_end):
        sent = [copy for when, copy in unsent if when is cond]

        def drain(sent=sent):
            for copy in sent:
                copy().wait_send()

        if cond is None:
            drain()
        else:
            pl.when(cond)(drain)
    assert len(keys) <= SEMS, len(keys)


def fused_body(tokens, expert_ids, combine_weights, w_gate, w_up, w_down):
    experts = lax.axis_size("expert")
    toks, width = tokens.shape
    top = expert_ids.shape[1]
    cap = min(toks, 5 * toks * top // (4 * experts))
    share, ff = w_down.shape[2], w_gate.shape[2]
    half = share // 2
    expert_iota = lax.broadcasted_iota(jnp.int32, (1, experts, 1), 1)
    chosen = expert_ids.T[:, None, :] == expert_iota
    table = jnp.sum(jnp.where(chosen, combine_weights.T[:, None, :], 0.0), axis=0)
    anywhere = pl.BlockSpec(memory_space=pl.ANY)
    inside = pl.BlockSpec(memory_space=pltpu.VMEM)
    n = LAYERS
    buffers = [
        pltpu.VMEM((n, toks, share), BF16),
        pltpu.VMEM((n, 2, toks, half), BF16),
        pltpu.VMEM((n, 4, cap, half), BF16),
        pltpu.VMEM((n, 4, cap, width), BF16),
        pltpu.VMEM((n, 4 * cap, 2 * ff), BF16),
        pltpu.VMEM((n, 4, cap, share), BF16),
        pltpu.VMEM((4 * cap, 128), F32),
        pltpu.VMEM((n, 4, experts, toks), F32),
        pltpu.VMEM((n, 4, experts, toks), jnp.int32),
        pltpu.VMEM((n, 4, 2 * cap, toks), BF16),
        pltpu.VMEM((n, 2, 2, cap, half), BF16),
        pltpu.VMEM((n, 2, toks, half), BF16),
        pltpu.VMEM((n, 2, toks, half), BF16),
        pltpu.VMEM((n - 1, toks, share), BF16),
        pltpu.VMEM((n - 1, toks, share), BF16),
        pltpu.VMEM((2, toks, share), BF16),
        pltpu.VMEM(w_gate.shape[1:], BF16),
        pltpu.VMEM(w_up.shape[1:], BF16),
        pltpu.VMEM(w_down.shape[1:], BF16),
    ]
    return pl.pallas_call(
        functools.partial(moe_kernel, cap),
        out_shape=jax.ShapeDtypeStruct((toks, share), BF16),
        in_specs=[anywhere, inside, anywhere, anywhere, anywhere],
        out_specs=inside,
        scratch_shapes=buffers + [
            pltpu.SemaphoreType.DMA((SEMS,)), pltpu.SemaphoreType.DMA((SEMS,)), pltpu.SemaphoreType.DMA((4,)),
        ],
        compiler_params=pltpu.CompilerParams(
            collective_id=0, has_side_effects=True, vmem_limit_bytes=60 * 1024 * 1024
        ),
    )(tokens, table, w_gate, w_up, w_down)


def split_dots(mine, weights):
    place = lax.axis_index("pipe")
    other = lax.ppermute(mine, "pipe", [(0, 1), (1, 0)])
    share = mine.shape[1]
    totals = []
    for weight in weights:
        own = lax.dynamic_slice_in_dim(weight, place * share, share, 0)
        far = lax.dynamic_slice_in_dim(weight, (1 - place) * share, share, 0)
        total = jnp.dot(mine, own, preferred_element_type=jnp.float32)
        totals.append(total + jnp.dot(other, far, preferred_element_type=jnp.float32))
    return totals


def body(tokens, expert_ids, combine_weights, w_gate, w_up, w_down):
    experts = lax.axis_size("expert")
    tok_rows, model_width = tokens.shape
    top_count = expert_ids.shape[1]
    capacity = min(tok_rows, 5 * tok_rows * top_count // (4 * experts))
    slot_count = experts * capacity
    out_width = w_down.shape[2]
    expert_iota = lax.broadcasted_iota(jnp.int32, (1, 1, experts), 2)
    chosen = (expert_ids[:, :, None] == expert_iota).astype(jnp.int32)
    expert_hits = jnp.sum(chosen, axis=1)
    earlier = lax.broadcasted_iota(jnp.int32, (tok_rows, tok_rows), 1)
    earlier = earlier < lax.broadcasted_iota(jnp.int32, (tok_rows, tok_rows), 0)
    rank_table = jnp.dot(
        earlier.astype(jnp.bfloat16), expert_hits.astype(jnp.bfloat16), preferred_element_type=jnp.float32
    ).astype(jnp.int32)
    slot_rank = jnp.sum(chosen * rank_table[:, None, :], axis=2)
    target = expert_ids * capacity + slot_rank
    slot_iota = lax.broadcasted_iota(jnp.int32, (1, 1, slot_count), 2)
    slot_marks = target[:, :, None] == slot_iota
    placing = jnp.any(slot_marks, axis=1).astype(jnp.bfloat16)
    blend_table = jnp.sum(jnp.where(slot_marks, combine_weights[:, :, None], 0.0), axis=1)
    pipes = lax.axis_size("pipe")
    place = lax.axis_index("pipe")
    width_share = model_width // pipes
    tok_share = lax.dynamic_slice_in_dim(tokens, place * width_share, width_share, 1)
    packed = jnp.einsum("ts,td->sd", placing, tok_share, preferred_element_type=jnp.float32)
    packed = packed.astype(jnp.bfloat16).reshape(experts, capacity, width_share)
    received = lax.all_to_all(packed, "expert", split_axis=0, concat_axis=0, tiled=True)
    rows = received.reshape(slot_count, width_share)
    if pipes == 2:
        gate_acc, up_acc = split_dots(rows, [w_gate[0], w_up[0]])
    else:
        rows = lax.all_gather(rows, "pipe", axis=1, tiled=True)
        gate_acc = jnp.dot(rows, w_gate[0], preferred_element_type=jnp.float32)
        up_acc = jnp.dot(rows, w_up[0], preferred_element_type=jnp.float32)
    hidden_rows = (jax.nn.silu(gate_acc) * up_acc).astype(jnp.bfloat16)
    if pipes == 2:
        (outputs,) = split_dots(hidden_rows, [w_down[0]])
    else:
        outputs = jnp.dot(
            lax.all_gather(hidden_rows, "pipe", axis=1, tiled=True),
            w_down[0],
            preferred_element_type=jnp.float32,
        )
    outgoing = outputs.astype(jnp.bfloat16).reshape(experts, capacity, out_width)
    returned_rows = lax.all_to_all(outgoing, "expert", split_axis=0, concat_axis=0, tiled=True)
    mixture = jnp.dot(
        blend_table,
        returned_rows.reshape(slot_count, out_width).astype(jnp.float32),
        precision=lax.Precision.HIGHEST,
        preferred_element_type=jnp.float32,
    )
    return mixture.astype(jnp.bfloat16)


def solution(mesh):
    placed = (
        P("expert", None),
        P("expert", None),
        P("expert", None),
        P("expert", None, "pipe"),
        P("expert", None, "pipe"),
        P("expert", None, "pipe"),
    )
    tree = mesh.shape["pipe"] == SIDE and mesh.shape["expert"] == LAYERS * SIDE * SIDE
    return jax.shard_map(
        fused_body if tree else body, mesh=mesh, in_specs=placed, out_specs=P("expert", "pipe"), check_vma=False
    )
```

```python
import functools
import jax
import jax.numpy as jnp
from jax import lax
from jax.experimental import pallas as pl
from jax.experimental.pallas import tpu as pltpu
from jax.sharding import PartitionSpec as P

LAYERS, SIDE = 4, 2
MESH = pl.DeviceIdType.MESH
BF16, F32 = jnp.bfloat16, jnp.float32
TILE = 256
SEMS = 176
IN, OUT = 0, 1


ORDER = (
    (("z0", 1), ("d1", 0, 0), ("d1", 0, 1), ("d2", 0, 0), ("d2", 0, 1), ("z0", 0), ("d3", 0, 0),),
    (("d1", 1, 1), ("r3", 1), ("d3", 0, 1), ("d1", 1, 0), ("d2", 1, 0), ("r3", 0), ("d2", 1, 1),),
    (("d3", 1, 0), ("d4", 0), ("d3", 1, 1), ("d1", 2, 1), ("gu", 0, 0, 1), ("d1", 2, 0), ("d4", 1),),
    (("d2", 2, 0), ("d2", 2, 1), ("gu", 1, 0, 1), ("d3", 2, 1), ("d3", 2, 0), ("d1", 3, 1), ("gu", 1, 1, 3),),
    (("d1", 3, 0), ("d2", 3, 1), ("d2", 3, 0), ("d4", 2), ("dn", 1), ("c1", 1, 0, 0), ("gu", 2, 0, 2),),
    (("d3", 3, 1), ("gu", 2, 2, 1), ("c1", 1, 1, 1), ("d3", 3, 0), ("c1", 1, 0, 1), ("gu", 2, 3, 1),),
    (("gu", 0, 1, 1), ("dn", 2), ("c1", 2, 1, 1), ("d4", 3), ("c2", 1, 1), ("c1", 1, 1, 0), ("c1", 2, 0, 1),),
    (("gu", 3, 0, 4), ("c1", 2, 1, 0), ("c2", 2, 1), ("dn", 3), ("c1", 3, 1, 1), ("c1", 3, 1, 0),),
    (("c1", 3, 0, 1), ("gu", 0, 2, 1), ("c3", 1, 1), ("gu", 0, 3, 1), ("c3", 2, 1), ("c2", 3, 1),),
    (("c1", 3, 0, 0), ("c2", 3, 0), ("dn", 0), ("c1", 0, 0, 1), ("c1", 2, 0, 0), ("c2", 2, 0), ("zm", 1, 1),),
    (("c1", 0, 1, 1), ("c3", 3, 1), ("c2", 1, 0), ("zm", 2, 1), ("c1", 0, 1, 0), ("c3", 3, 0), ("c3", 2, 0),),
    (("zm", 2, 0), ("zm", 3, 1), ("c2", 0, 1), ("c2", 0, 0), ("c3", 1, 0), ("c1", 0, 0, 0), ("zm", 1, 0),),
    (("zm", 3, 0), ("c3", 0, 1), ("fin", 1), ("c3", 0, 0), ("fin", 0),),
)

def moe_kernel(
    cap, tok_hbm, table_ref, wg_hbm, wu_hbm, wd_hbm, out_ref,
    full, first, leaf, rows, hidden, outs, row_weight, tabs, slots, marks,
    trim, sums_out, sums_in, zsend, zpass, zfin, wg, wu, wd,
    send_sem, recv_sem, local_sem,
):
    p = lax.axis_index("pipe")
    me = lax.axis_index("expert")
    z, y, x = me // 4, lax.rem(me // 2, 2), lax.rem(me, 2)
    toks, share = full.shape[1:]
    half = share // 2
    ff = wg.shape[1]
    base = pl.multiple_of(p * share, 128)
    mid = lax.rem((z + 1) // 2, 2)
    is_mid, is_end = mid == 1, mid == 0
    step = 1 - 2 * (z // 2)

    def chip(zz, yy, xx):
        return {"pipe": p, "expert": zz * 4 + yy * 2 + xx}

    xn, yn, dn = chip(z, y, 1 - x), chip(z, 1 - y, x), chip(z, 1 - y, 1 - x)
    inward = chip(z + step, y, x)
    outward = chip(z - step * mid, y, x)
    twin = {"pipe": 1 - p, "expert": me}
    layer = z * 4
    e_x, e_y = layer + y * 2 + 1 - x, layer + (1 - y) * 2 + x
    g_me, g_y, g_x, g_d = y * 2 + x, (1 - y) * 2 + x, y * 2 + 1 - x, (1 - y) * 2 + 1 - x

    keys = {}
    unsent = []

    def sem(*key):
        return keys.setdefault(key, len(keys))

    def make(skey, rkey, source, slot, device):
        source, slot = (ref() if callable(ref) else ref for ref in (source, slot))
        return pltpu.make_async_remote_copy(
            src_ref=source, dst_ref=slot, send_sem=send_sem.at[sem("s", *skey)],
            recv_sem=recv_sem.at[sem("s", *rkey)], device_id=device, device_id_type=MESH,
        )

    def send(skey, rkey, source, slot, device, when=None):
        make(skey, rkey, source, slot, device).start()
        unsent.append((when, functools.partial(make, skey, rkey, source, slot, device)))

    def arrived(rkey, slot):
        make(rkey, rkey, slot, slot, xn).wait_recv()

    def cols(h):
        return pl.ds(h * half, half)

    def wide_cols(h):
        return pl.ds(pl.multiple_of(base + h * half, 128), half)

    def load_tokens():
        return pltpu.make_async_copy(tok_hbm.at[:, pl.ds(base, share)], full.at[0], local_sem.at[3])

    weight_loads = [
        pltpu.make_async_copy(wg_hbm.at[0], wg, local_sem.at[0]),
        pltpu.make_async_copy(wu_hbm.at[0], wu, local_sem.at[1]),
        pltpu.make_async_copy(wd_hbm.at[0], wd, local_sem.at[2]),
    ]
    load_tokens().start()
    barrier = pltpu.get_barrier_semaphore()
    for device in (xn, yn, dn, twin, inward):
        pl.semaphore_signal(barrier, inc=1, device_id=device, device_id_type=MESH)

    @pl.when(is_mid)
    def _():
        pl.semaphore_signal(barrier, inc=1, device_id=outward, device_id_type=MESH)

    for copy in weight_loads:
        copy.start()
    tabs[0, g_me] = table_ref[...]

    def earlier():
        a = lax.broadcasted_iota(jnp.int32, (toks, toks), 0)
        return jnp.where(a < lax.broadcasted_iota(jnp.int32, (toks, toks), 1), 1.0, 0.0).astype(BF16)

    def rank(c, g):
        table = tabs[c, g]
        named = table > 0.0
        order = jnp.dot(jnp.where(named, 1.0, 0.0).astype(BF16), earlier(), preferred_element_type=F32)
        slots[c, g] = jnp.where(named, order.astype(jnp.int32), -1)

    def picks(c, g, e):
        place = slots[c, g, pl.ds(e, 1), :]
        return place == lax.broadcasted_iota(jnp.int32, (cap, toks), 0)

    def mark(c, k, g, other):
        marks[c, k, pl.ds(0, cap)] = jnp.where(picks(c, g, me), 1.0, 0.0).astype(BF16)
        marks[c, k, pl.ds(cap, cap)] = jnp.where(picks(c, g, other), 1.0, 0.0).astype(BF16)

    rank(0, g_me)
    pl.semaphore_wait(barrier, 5 + mid)
    load_tokens().wait()

    def z_hop(name, c, target, device, h, when):
        send(
            (name, h), ("zf", target, h), lambda: full.at[c, :, cols(h)],
            lambda: full.at[target, :, cols(h)], device, when,
        )
        if h == 0:
            send(
                (name, "t"), ("zf", target, "t"), lambda: tabs.at[c, g_me],
                lambda: tabs.at[target, g_me], device, when,
            )

    def z0(h):
        @pl.when(is_mid)
        def _():
            z_hop("own", 0, 1, inward, h, is_mid)
            z_hop("own_out", 0, 1, outward, h, is_mid)

        @pl.when(is_end)
        def _():
            z_hop("own_end", 0, 3, inward, h, is_end)

    def z_wait(c, h):
        arrived(("zf", c, h), full.at[c, :, cols(h)])
        if h == 0:
            arrived(("zf", c, "t"), tabs.at[c, g_me])

    def r3(h):
        @pl.when(is_mid)
        def _():
            z_wait(3, h)
            z_hop("pass3", 3, 2, inward, h, is_mid)

    def share_table(c):
        for name, device in (("y", yn), ("x", xn), ("d", dn)):
            key = ("tab" + name, c)
            send(key, key, tabs.at[c, g_me], tabs.at[c, g_me], device)

    def d1(c, h):
        if c in (1, 2):
            z_wait(c, h)

            @pl.when(is_mid)
            def _():
                z_hop(f"pass{c}", c, c + 1, outward, h, is_mid)
        if c == 3:
            @pl.when(is_end)
            def _():
                z_wait(3, h)
        if h == 0:
            share_table(c)
        key = ("first", c, h)
        send(key, key, full.at[c, :, cols(h)], first.at[c, h], xn if h else yn)

    def pack(c, k, h, g, source, device):
        packed = jnp.dot(marks[c, k], source, preferred_element_type=F32).astype(BF16)
        rows[c, g, :, wide_cols(h)] = packed[:cap]
        leaf[c, k] = packed[cap:]
        key = ("leaf", c, k)
        send(key, key, leaf.at[c, k], rows.at[c, g, :, wide_cols(h)], device)

    ready = {(0, "me")}

    def ranked(c, name, g):
        if (c, name) not in ready:
            ready.add((c, name))
            if name != "me":
                arrived(("tab" + name, c), tabs.at[c, g])
            rank(c, g)

    def d2(c, h):
        ranked(c, "me", g_me)
        mark(c, h, g_me, e_y if h else e_x)
        pack(c, h, h, g_me, full[c, :, cols(h)], yn if h else xn)

    def d3(c, h):
        name, g = ("x", g_x) if h else ("y", g_y)
        ranked(c, name, g)
        mark(c, 2 + h, g, e_y if h else e_x)
        arrived(("first", c, h), first.at[c, h])
        pack(c, 2 + h, h, g, first[c, h], yn if h else xn)

    def d4(c):
        for k, g, h in ((0, g_x, 0), (1, g_y, 1), (2, g_d, 0), (3, g_d, 1)):
            arrived(("leaf", c, k), rows.at[c, g, :, wide_cols(h)])
        mine = rows.at[c, :, :, pl.ds(base, share)]
        send(("twin", c), ("twin", c), mine, mine, twin)

    def twin_hidden(c, n):
        tile = hidden.at[c, :, pl.ds(pl.multiple_of(p * ff + n * TILE, TILE), TILE)]
        at = sem("s", "hidden", c, 0) + n
        return pltpu.make_async_remote_copy(
            src_ref=tile, dst_ref=tile, send_sem=send_sem.at[at], recv_sem=recv_sem.at[at],
            device_id=twin, device_id_type=MESH,
        )

    ff_tiles = ff // TILE

    loaded = set()

    def weights(*which):
        for i in which:
            if i not in loaded:
                loaded.add(i)
                weight_loads[i].wait()

    def gu(c, first_tile, tiles):
        for n in range(ff_tiles):
            sem("s", "hidden", c, n)
        if first_tile == 0:
            arrived(("twin", c), rows.at[c, :, :, pl.ds(0, share)])
        weights(0, 1)

        def tile(n, carry):
            at = pl.ds(pl.multiple_of(n * TILE, TILE), TILE)
            mine = rows[c].reshape(4 * cap, 2 * share)
            gate = jnp.dot(mine, wg[:, at], preferred_element_type=F32)
            up = jnp.dot(mine, wu[:, at], preferred_element_type=F32)
            value = (gate / (1.0 + jnp.exp(-gate)) * up).astype(BF16)
            hidden[c, :, pl.ds(pl.multiple_of(p * ff + n * TILE, TILE), TILE)] = value
            twin_hidden(c, n).start()
            return carry

        lax.fori_loop(first_tile, first_tile + tiles, tile, 0)

    def dn_(c):
        ranked(c, "d", g_d)
        for g in range(4):
            weight = tabs[c, g, pl.ds(me, 1), :]
            column = jnp.sum(jnp.where(picks(c, g, me), weight, 0.0), axis=1, keepdims=True)
            row_weight[pl.ds(g * cap, cap)] = jnp.broadcast_to(column, (cap, 128))
        weights(2)

        def landed(n, carry):
            twin_hidden(c, n).wait_recv()
            return carry

        lax.fori_loop(0, ff_tiles, landed, 0)

        def tile(n, carry):
            at = pl.ds(pl.multiple_of(n * TILE, TILE), TILE)
            value = jnp.dot(hidden[c], wd[:, at], preferred_element_type=F32)
            scale = row_weight[...]
            value = value * jnp.concatenate([scale] * (TILE // 128), axis=1)
            outs[c, :, :, at] = value.astype(BF16).reshape(4, cap, TILE)
            return carry

        lax.fori_loop(0, share // TILE, tile, 0)

    def c1(c, h, j):
        g = g_d if j else (g_y if h else g_x)
        key = ("trim", c, h, j)
        send(key, key, outs.at[c, g, :, cols(h)], trim.at[c, h, j], yn if h else xn)

    def spread(c, k, g, h, j):
        arrived(("trim", c, h, j), trim.at[c, h, j])
        dims = (((0,), (0,)), ((), ()))
        one = lax.dot_general(marks[c, k, pl.ds(0, cap)], outs[c, g, :, cols(h)], dims, preferred_element_type=F32)
        return one + lax.dot_general(marks[c, k, pl.ds(cap, cap)], trim[c, h, j], dims, preferred_element_type=F32)

    def c2(c, h):
        sums_out[c, h] = spread(c, 2 + h, g_x if h else g_y, h, 1).astype(BF16)
        key = ("sums", c, h)
        send(key, key, sums_out.at[c, h], sums_in.at[c, h], xn if h else yn)

    def layer_sum(c, h):
        value = spread(c, h, g_me, h, 0)
        arrived(("sums", c, h), sums_in.at[c, h])
        return value + sums_in[c, h].astype(F32)

    def z_sum(name, c, h, target, device, when):
        buffer, at = target
        send(
            (name, c, h), ("zpass" if buffer is zpass else "zfin", at, h),
            lambda: zsend.at[c - 1, :, cols(h)], lambda: buffer.at[at, :, cols(h)], device, when,
        )

    own = {}

    def c3(c, h):
        value = layer_sum(c, h)
        if c == 0:
            own[h] = value
            return
        zsend[c - 1, :, cols(h)] = value.astype(BF16)

        @pl.when(is_end)
        def _():
            z_sum("zend", c, h, (zfin, OUT) if c == 1 else (zpass, c - 2), inward, is_end)

    def zm(c, h):
        @pl.when(is_mid)
        def _():
            arrived(("zpass", c - 1, h), zpass.at[c - 1, :, cols(h)])
            total = zsend[c - 1, :, cols(h)].astype(F32) + zpass[c - 1, :, cols(h)].astype(F32)
            zsend[c - 1, :, cols(h)] = total.astype(BF16)
            z_sum("zmid", c, h, (zpass, 2) if c == 2 else (zfin, IN), outward if c == 3 else inward, is_mid)

    def fin(h):
        arrived(("zfin", IN, h), zfin.at[IN, :, cols(h)])

        @pl.when(is_mid)
        def _():
            arrived(("zfin", OUT, h), zfin.at[OUT, :, cols(h)])
            value = own[h] + zfin[IN, :, cols(h)].astype(F32) + zfin[OUT, :, cols(h)].astype(F32)
            out_ref[:, cols(h)] = value.astype(BF16)

        @pl.when(is_end)
        def _():
            out_ref[:, cols(h)] = (own[h] + zfin[IN, :, cols(h)].astype(F32)).astype(BF16)

    step_of = {
        "z0": z0, "r3": r3, "d1": d1, "d2": d2, "d3": d3, "d4": d4, "gu": gu, "dn": dn_,
        "c1": c1, "c2": c2, "c3": c3, "zm": zm, "fin": fin,
    }
    for entry in ORDER:
        for name, *numbers in entry:
            step_of[name](*numbers)
    for c in range(4):
        for n in range(ff_tiles):
            sem("s", "hidden", c, n)

    for c in range(4):
        lax.fori_loop(0, ff_tiles, lambda n, carry, c=c: (twin_hidden(c, n).wait_send(), carry)[1], 0)
    for cond in (None, is_mid, is_end):
        sent = [copy for when, copy in unsent if when is cond]

        def drain(sent=sent):
            for copy in sent:
                copy().wait_send()

        if cond is None:
            drain()
        else:
            pl.when(cond)(drain)
    assert len(keys) <= SEMS, len(keys)


def fused_body(tokens, expert_ids, combine_weights, w_gate, w_up, w_down):
    experts = lax.axis_size("expert")
    toks, width = tokens.shape
    top = expert_ids.shape[1]
    cap = min(toks, 5 * toks * top // (4 * experts))
    share, ff = w_down.shape[2], w_gate.shape[2]
    half = share // 2
    expert_iota = lax.broadcasted_iota(jnp.int32, (1, experts, 1), 1)
    chosen = expert_ids.T[:, None, :] == expert_iota
    table = jnp.sum(jnp.where(chosen, combine_weights.T[:, None, :], 0.0), axis=0)
    anywhere = pl.BlockSpec(memory_space=pl.ANY)
    inside = pl.BlockSpec(memory_space=pltpu.VMEM)
    n = LAYERS
    buffers = [
        pltpu.VMEM((n, toks, share), BF16),
        pltpu.VMEM((n, 2, toks, half), BF16),
        pltpu.VMEM((n, 4, cap, half), BF16),
        pltpu.VMEM((n, 4, cap, width), BF16),
        pltpu.VMEM((n, 4 * cap, 2 * ff), BF16),
        pltpu.VMEM((n, 4, cap, share), BF16),
        pltpu.VMEM((4 * cap, 128), F32),
        pltpu.VMEM((n, 4, experts, toks), F32),
        pltpu.VMEM((n, 4, experts, toks), jnp.int32),
        pltpu.VMEM((n, 4, 2 * cap, toks), BF16),
        pltpu.VMEM((n, 2, 2, cap, half), BF16),
        pltpu.VMEM((n, 2, toks, half), BF16),
        pltpu.VMEM((n, 2, toks, half), BF16),
        pltpu.VMEM((n - 1, toks, share), BF16),
        pltpu.VMEM((n - 1, toks, share), BF16),
        pltpu.VMEM((2, toks, share), BF16),
        pltpu.VMEM(w_gate.shape[1:], BF16),
        pltpu.VMEM(w_up.shape[1:], BF16),
        pltpu.VMEM(w_down.shape[1:], BF16),
    ]
    return pl.pallas_call(
        functools.partial(moe_kernel, cap),
        out_shape=jax.ShapeDtypeStruct((toks, share), BF16),
        in_specs=[anywhere, inside, anywhere, anywhere, anywhere],
        out_specs=inside,
        scratch_shapes=buffers + [
            pltpu.SemaphoreType.DMA((SEMS,)), pltpu.SemaphoreType.DMA((SEMS,)), pltpu.SemaphoreType.DMA((4,)),
        ],
        compiler_params=pltpu.CompilerParams(
            collective_id=0, has_side_effects=True, vmem_limit_bytes=60 * 1024 * 1024
        ),
    )(tokens, table, w_gate, w_up, w_down)


def split_dots(mine, weights):
    place = lax.axis_index("pipe")
    other = lax.ppermute(mine, "pipe", [(0, 1), (1, 0)])
    share = mine.shape[1]
    totals = []
    for weight in weights:
        own = lax.dynamic_slice_in_dim(weight, place * share, share, 0)
        far = lax.dynamic_slice_in_dim(weight, (1 - place) * share, share, 0)
        total = jnp.dot(mine, own, preferred_element_type=jnp.float32)
        totals.append(total + jnp.dot(other, far, preferred_element_type=jnp.float32))
    return totals


def body(tokens, expert_ids, combine_weights, w_gate, w_up, w_down):
    experts = lax.axis_size("expert")
    tok_rows, model_width = tokens.shape
    top_count = expert_ids.shape[1]
    capacity = min(tok_rows, 5 * tok_rows * top_count // (4 * experts))
    slot_count = experts * capacity
    out_width = w_down.shape[2]
    expert_iota = lax.broadcasted_iota(jnp.int32, (1, 1, experts), 2)
    chosen = (expert_ids[:, :, None] == expert_iota).astype(jnp.int32)
    expert_hits = jnp.sum(chosen, axis=1)
    earlier = lax.broadcasted_iota(jnp.int32, (tok_rows, tok_rows), 1)
    earlier = earlier < lax.broadcasted_iota(jnp.int32, (tok_rows, tok_rows), 0)
    rank_table = jnp.dot(
        earlier.astype(jnp.bfloat16), expert_hits.astype(jnp.bfloat16), preferred_element_type=jnp.float32
    ).astype(jnp.int32)
    slot_rank = jnp.sum(chosen * rank_table[:, None, :], axis=2)
    target = expert_ids * capacity + slot_rank
    slot_iota = lax.broadcasted_iota(jnp.int32, (1, 1, slot_count), 2)
    slot_marks = target[:, :, None] == slot_iota
    placing = jnp.any(slot_marks, axis=1).astype(jnp.bfloat16)
    blend_table = jnp.sum(jnp.where(slot_marks, combine_weights[:, :, None], 0.0), axis=1)
    pipes = lax.axis_size("pipe")
    place = lax.axis_index("pipe")
    width_share = model_width // pipes
    tok_share = lax.dynamic_slice_in_dim(tokens, place * width_share, width_share, 1)
    packed = jnp.einsum("ts,td->sd", placing, tok_share, preferred_element_type=jnp.float32)
    packed = packed.astype(jnp.bfloat16).reshape(experts, capacity, width_share)
    received = lax.all_to_all(packed, "expert", split_axis=0, concat_axis=0, tiled=True)
    rows = received.reshape(slot_count, width_share)
    if pipes == 2:
        gate_acc, up_acc = split_dots(rows, [w_gate[0], w_up[0]])
    else:
        rows = lax.all_gather(rows, "pipe", axis=1, tiled=True)
        gate_acc = jnp.dot(rows, w_gate[0], preferred_element_type=jnp.float32)
        up_acc = jnp.dot(rows, w_up[0], preferred_element_type=jnp.float32)
    hidden_rows = (jax.nn.silu(gate_acc) * up_acc).astype(jnp.bfloat16)
    if pipes == 2:
        (outputs,) = split_dots(hidden_rows, [w_down[0]])
    else:
        outputs = jnp.dot(
            lax.all_gather(hidden_rows, "pipe", axis=1, tiled=True),
            w_down[0],
            preferred_element_type=jnp.float32,
        )
    outgoing = outputs.astype(jnp.bfloat16).reshape(experts, capacity, out_width)
    returned_rows = lax.all_to_all(outgoing, "expert", split_axis=0, concat_axis=0, tiled=True)
    mixture = jnp.dot(
        blend_table,
        returned_rows.reshape(slot_count, out_width).astype(jnp.float32),
        precision=lax.Precision.HIGHEST,
        preferred_element_type=jnp.float32,
    )
    return mixture.astype(jnp.bfloat16)


def solution(mesh):
    placed = (
        P("expert", None),
        P("expert", None),
        P("expert", None),
        P("expert", None, "pipe"),
        P("expert", None, "pipe"),
        P("expert", None, "pipe"),
    )
    tree = mesh.shape["pipe"] == SIDE and mesh.shape["expert"] == LAYERS * SIDE * SIDE
    return jax.shard_map(
        fused_body if tree else body, mesh=mesh, in_specs=placed, out_specs=P("expert", "pipe"), check_vma=False
    )
```

```python
import functools
import jax
import jax.numpy as jnp
from jax import lax
from jax.experimental import pallas as pl
from jax.experimental.pallas import tpu as pltpu
from jax.sharding import PartitionSpec as P

LAYERS, SIDE = 4, 2
MESH = pl.DeviceIdType.MESH
BF16, F32 = jnp.bfloat16, jnp.float32
TILE = 256
SEMS = 176
IN, OUT = 0, 1


ORDER = (
    (("d1", 0, 0), ("d1", 0, 1), ("z0", 0), ("d2", 0, 1), ("z0", 1), ("d2", 0, 0), ("d3", 0, 0), ("r3", 0),),
    (("d1", 1, 0), ("d3", 0, 1), ("d1", 1, 1), ("d2", 1, 1), ("d3", 1, 0), ("r3", 1), ("d2", 1, 0),),
    (("d3", 1, 1), ("d4", 0), ("d1", 2, 0), ("d1", 2, 1), ("d2", 2, 1), ("gu", 0, 0, 1), ("d4", 1),),
    (("gu", 0, 1, 1), ("d2", 2, 0), ("gu", 1, 0, 2), ("d1", 3, 0), ("d3", 2, 0), ("gu", 1, 2, 2),),
    (("d3", 2, 1), ("d1", 3, 1), ("d2", 3, 1), ("dn", 1), ("d3", 3, 0), ("c1", 1, 1, 1), ("d4", 2),),
    (("d2", 3, 0), ("d3", 3, 1), ("gu", 2, 0, 4), ("c2", 1, 1), ("d4", 3), ("dn", 2), ("c1", 2, 1, 1),),
    (("c1", 1, 0, 0), ("c1", 2, 0, 1), ("gu", 3, 0, 2), ("c1", 1, 1, 0), ("gu", 3, 2, 2), ("c1", 2, 1, 0),),
    (("c2", 2, 1), ("dn", 3), ("c1", 3, 1, 1), ("c1", 3, 1, 0), ("c1", 3, 0, 1), ("c3", 1, 1),),
    (("gu", 0, 2, 2), ("c2", 3, 1), ("c3", 2, 1), ("c1", 3, 0, 0), ("c1", 1, 0, 1), ("c2", 3, 0), ("dn", 0),),
    (("c1", 2, 0, 0), ("c3", 3, 1), ("c1", 0, 0, 1), ("c1", 0, 1, 1), ("zm", 1, 1), ("c2", 2, 0),),
    (("zm", 2, 1), ("c3", 3, 0), ("c2", 1, 0), ("c3", 2, 0), ("zm", 2, 0), ("c1", 0, 1, 0), ("c2", 0, 1),),
    (("zm", 3, 1), ("c2", 0, 0), ("c3", 1, 0), ("c1", 0, 0, 0), ("zm", 1, 0), ("zm", 3, 0), ("c3", 0, 1),),
    (("fin", 1), ("c3", 0, 0), ("fin", 0),),
)

def moe_kernel(
    cap, tok_hbm, table_ref, wg_hbm, wu_hbm, wd_hbm, out_ref,
    full, first, leaf, rows, hidden, outs, row_weight, tabs, slots, marks,
    trim, sums_out, sums_in, zsend, zpass, zfin, wg, wu, wd,
    send_sem, recv_sem, local_sem,
):
    p = lax.axis_index("pipe")
    me = lax.axis_index("expert")
    z, y, x = me // 4, lax.rem(me // 2, 2), lax.rem(me, 2)
    toks, share = full.shape[1:]
    half = share // 2
    ff = wg.shape[1]
    base = pl.multiple_of(p * share, 128)
    mid = lax.rem((z + 1) // 2, 2)
    is_mid, is_end = mid == 1, mid == 0
    step = 1 - 2 * (z // 2)

    def chip(zz, yy, xx):
        return {"pipe": p, "expert": zz * 4 + yy * 2 + xx}

    xn, yn, dn = chip(z, y, 1 - x), chip(z, 1 - y, x), chip(z, 1 - y, 1 - x)
    inward = chip(z + step, y, x)
    outward = chip(z - step * mid, y, x)
    twin = {"pipe": 1 - p, "expert": me}
    layer = z * 4
    e_x, e_y = layer + y * 2 + 1 - x, layer + (1 - y) * 2 + x
    g_me, g_y, g_x, g_d = y * 2 + x, (1 - y) * 2 + x, y * 2 + 1 - x, (1 - y) * 2 + 1 - x

    keys = {}
    unsent = []

    def sem(*key):
        return keys.setdefault(key, len(keys))

    def make(skey, rkey, source, slot, device):
        source, slot = (ref() if callable(ref) else ref for ref in (source, slot))
        return pltpu.make_async_remote_copy(
            src_ref=source, dst_ref=slot, send_sem=send_sem.at[sem("s", *skey)],
            recv_sem=recv_sem.at[sem("s", *rkey)], device_id=device, device_id_type=MESH,
        )

    def send(skey, rkey, source, slot, device, when=None):
        make(skey, rkey, source, slot, device).start()
        unsent.append((when, functools.partial(make, skey, rkey, source, slot, device)))

    def arrived(rkey, slot):
        make(rkey, rkey, slot, slot, xn).wait_recv()

    def cols(h):
        return pl.ds(h * half, half)

    def wide_cols(h):
        return pl.ds(pl.multiple_of(base + h * half, 128), half)

    def load_tokens():
        return pltpu.make_async_copy(tok_hbm.at[:, pl.ds(base, share)], full.at[0], local_sem.at[3])

    weight_loads = [
        pltpu.make_async_copy(wg_hbm.at[0], wg, local_sem.at[0]),
        pltpu.make_async_copy(wu_hbm.at[0], wu, local_sem.at[1]),
        pltpu.make_async_copy(wd_hbm.at[0], wd, local_sem.at[2]),
    ]
    load_tokens().start()
    barrier = pltpu.get_barrier_semaphore()
    for device in (xn, yn, dn, twin, inward):
        pl.semaphore_signal(barrier, inc=1, device_id=device, device_id_type=MESH)

    @pl.when(is_mid)
    def _():
        pl.semaphore_signal(barrier, inc=1, device_id=outward, device_id_type=MESH)

    for copy in weight_loads:
        copy.start()
    tabs[0, g_me] = table_ref[...]

    def earlier():
        a = lax.broadcasted_iota(jnp.int32, (toks, toks), 0)
        return jnp.where(a < lax.broadcasted_iota(jnp.int32, (toks, toks), 1), 1.0, 0.0).astype(BF16)

    def rank(c, g):
        table = tabs[c, g]
        named = table > 0.0
        order = jnp.dot(jnp.where(named, 1.0, 0.0).astype(BF16), earlier(), preferred_element_type=F32)
        slots[c, g] = jnp.where(named, order.astype(jnp.int32), -1)

    def picks(c, g, e):
        place = slots[c, g, pl.ds(e, 1), :]
        return place == lax.broadcasted_iota(jnp.int32, (cap, toks), 0)

    def mark(c, k, g, other):
        marks[c, k, pl.ds(0, cap)] = jnp.where(picks(c, g, me), 1.0, 0.0).astype(BF16)
        marks[c, k, pl.ds(cap, cap)] = jnp.where(picks(c, g, other), 1.0, 0.0).astype(BF16)

    rank(0, g_me)
    pl.semaphore_wait(barrier, 5 + mid)
    load_tokens().wait()

    def z_hop(name, c, target, device, h, when):
        send(
            (name, h), ("zf", target, h), lambda: full.at[c, :, cols(h)],
            lambda: full.at[target, :, cols(h)], device, when,
        )
        if h == 0:
            send(
                (name, "t"), ("zf", target, "t"), lambda: tabs.at[c, g_me],
                lambda: tabs.at[target, g_me], device, when,
            )

    def z0(h):
        @pl.when(is_mid)
        def _():
            z_hop("own", 0, 1, inward, h, is_mid)
            z_hop("own_out", 0, 1, outward, h, is_mid)

        @pl.when(is_end)
        def _():
            z_hop("own_end", 0, 3, inward, h, is_end)

    def z_wait(c, h):
        arrived(("zf", c, h), full.at[c, :, cols(h)])
        if h == 0:
            arrived(("zf", c, "t"), tabs.at[c, g_me])

    def r3(h):
        @pl.when(is_mid)
        def _():
            z_wait(3, h)
            z_hop("pass3", 3, 2, inward, h, is_mid)

    def share_table(c):
        for name, device in (("y", yn), ("x", xn), ("d", dn)):
            key = ("tab" + name, c)
            send(key, key, tabs.at[c, g_me], tabs.at[c, g_me], device)

    def d1(c, h):
        if c in (1, 2):
            z_wait(c, h)

            @pl.when(is_mid)
            def _():
                z_hop(f"pass{c}", c, c + 1, outward, h, is_mid)
        if c == 3:
            @pl.when(is_end)
            def _():
                z_wait(3, h)
        if h == 0:
            share_table(c)
        key = ("first", c, h)
        send(key, key, full.at[c, :, cols(h)], first.at[c, h], xn if h else yn)

    def pack(c, k, h, g, source, device):
        packed = jnp.dot(marks[c, k], source, preferred_element_type=F32).astype(BF16)
        rows[c, g, :, wide_cols(h)] = packed[:cap]
        leaf[c, k] = packed[cap:]
        key = ("leaf", c, k)
        send(key, key, leaf.at[c, k], rows.at[c, g, :, wide_cols(h)], device)

    ready = {(0, "me")}

    def ranked(c, name, g):
        if (c, name) not in ready:
            ready.add((c, name))
            if name != "me":
                arrived(("tab" + name, c), tabs.at[c, g])
            rank(c, g)

    def d2(c, h):
        ranked(c, "me", g_me)
        mark(c, h, g_me, e_y if h else e_x)
        pack(c, h, h, g_me, full[c, :, cols(h)], yn if h else xn)

    def d3(c, h):
        name, g = ("x", g_x) if h else ("y", g_y)
        ranked(c, name, g)
        mark(c, 2 + h, g, e_y if h else e_x)
        arrived(("first", c, h), first.at[c, h])
        pack(c, 2 + h, h, g, first[c, h], yn if h else xn)

    def d4(c):
        for k, g, h in ((0, g_x, 0), (1, g_y, 1), (2, g_d, 0), (3, g_d, 1)):
            arrived(("leaf", c, k), rows.at[c, g, :, wide_cols(h)])
        mine = rows.at[c, :, :, pl.ds(base, share)]
        send(("twin", c), ("twin", c), mine, mine, twin)

    def twin_hidden(c, n):
        tile = hidden.at[c, :, pl.ds(pl.multiple_of(p * ff + n * TILE, TILE), TILE)]
        at = sem("s", "hidden", c, 0) + n
        return pltpu.make_async_remote_copy(
            src_ref=tile, dst_ref=tile, send_sem=send_sem.at[at], recv_sem=recv_sem.at[at],
            device_id=twin, device_id_type=MESH,
        )

    ff_tiles = ff // TILE

    loaded = set()

    def weights(*which):
        for i in which:
            if i not in loaded:
                loaded.add(i)
                weight_loads[i].wait()

    def gu(c, first_tile, tiles):
        for n in range(ff_tiles):
            sem("s", "hidden", c, n)
        if first_tile == 0:
            arrived(("twin", c), rows.at[c, :, :, pl.ds(0, share)])
        weights(0, 1)

        def tile(n, carry):
            at = pl.ds(pl.multiple_of(n * TILE, TILE), TILE)
            mine = rows[c].reshape(4 * cap, 2 * share)
            gate = jnp.dot(mine, wg[:, at], preferred_element_type=F32)
            up = jnp.dot(mine, wu[:, at], preferred_element_type=F32)
            value = (gate / (1.0 + jnp.exp(-gate)) * up).astype(BF16)
            hidden[c, :, pl.ds(pl.multiple_of(p * ff + n * TILE, TILE), TILE)] = value
            twin_hidden(c, n).start()
            return carry

        lax.fori_loop(first_tile, first_tile + tiles, tile, 0)

    def dn_(c):
        ranked(c, "d", g_d)
        for g in range(4):
            weight = tabs[c, g, pl.ds(me, 1), :]
            column = jnp.sum(jnp.where(picks(c, g, me), weight, 0.0), axis=1, keepdims=True)
            row_weight[pl.ds(g * cap, cap)] = jnp.broadcast_to(column, (cap, 128))
        weights(2)

        def landed(n, carry):
            twin_hidden(c, n).wait_recv()
            return carry

        lax.fori_loop(0, ff_tiles, landed, 0)

        def tile(n, carry):
            at = pl.ds(pl.multiple_of(n * TILE, TILE), TILE)
            value = jnp.dot(hidden[c], wd[:, at], preferred_element_type=F32)
            scale = row_weight[...]
            value = value * jnp.concatenate([scale] * (TILE // 128), axis=1)
            outs[c, :, :, at] = value.astype(BF16).reshape(4, cap, TILE)
            return carry

        lax.fori_loop(0, share // TILE, tile, 0)

    def c1(c, h, j):
        g = g_d if j else (g_y if h else g_x)
        key = ("trim", c, h, j)
        send(key, key, outs.at[c, g, :, cols(h)], trim.at[c, h, j], yn if h else xn)

    def spread(c, k, g, h, j):
        arrived(("trim", c, h, j), trim.at[c, h, j])
        dims = (((0,), (0,)), ((), ()))
        one = lax.dot_general(marks[c, k, pl.ds(0, cap)], outs[c, g, :, cols(h)], dims, preferred_element_type=F32)
        return one + lax.dot_general(marks[c, k, pl.ds(cap, cap)], trim[c, h, j], dims, preferred_element_type=F32)

    def c2(c, h):
        sums_out[c, h] = spread(c, 2 + h, g_x if h else g_y, h, 1).astype(BF16)
        key = ("sums", c, h)
        send(key, key, sums_out.at[c, h], sums_in.at[c, h], xn if h else yn)

    def layer_sum(c, h):
        value = spread(c, h, g_me, h, 0)
        arrived(("sums", c, h), sums_in.at[c, h])
        return value + sums_in[c, h].astype(F32)

    def z_sum(name, c, h, target, device, when):
        buffer, at = target
        send(
            (name, c, h), ("zpass" if buffer is zpass else "zfin", at, h),
            lambda: zsend.at[c - 1, :, cols(h)], lambda: buffer.at[at, :, cols(h)], device, when,
        )

    own = {}

    def c3(c, h):
        value = layer_sum(c, h)
        if c == 0:
            own[h] = value
            return
        zsend[c - 1, :, cols(h)] = value.astype(BF16)

        @pl.when(is_end)
        def _():
            z_sum("zend", c, h, (zfin, OUT) if c == 1 else (zpass, c - 2), inward, is_end)

    def zm(c, h):
        @pl.when(is_mid)
        def _():
            arrived(("zpass", c - 1, h), zpass.at[c - 1, :, cols(h)])
            total = zsend[c - 1, :, cols(h)].astype(F32) + zpass[c - 1, :, cols(h)].astype(F32)
            zsend[c - 1, :, cols(h)] = total.astype(BF16)
            z_sum("zmid", c, h, (zpass, 2) if c == 2 else (zfin, IN), outward if c == 3 else inward, is_mid)

    def fin(h):
        arrived(("zfin", IN, h), zfin.at[IN, :, cols(h)])

        @pl.when(is_mid)
        def _():
            arrived(("zfin", OUT, h), zfin.at[OUT, :, cols(h)])
            value = own[h] + zfin[IN, :, cols(h)].astype(F32) + zfin[OUT, :, cols(h)].astype(F32)
            out_ref[:, cols(h)] = value.astype(BF16)

        @pl.when(is_end)
        def _():
            out_ref[:, cols(h)] = (own[h] + zfin[IN, :, cols(h)].astype(F32)).astype(BF16)

    step_of = {
        "z0": z0, "r3": r3, "d1": d1, "d2": d2, "d3": d3, "d4": d4, "gu": gu, "dn": dn_,
        "c1": c1, "c2": c2, "c3": c3, "zm": zm, "fin": fin,
    }
    for entry in ORDER:
        for name, *numbers in entry:
            step_of[name](*numbers)
    for c in range(4):
        for n in range(ff_tiles):
            sem("s", "hidden", c, n)

    for c in range(4):
        lax.fori_loop(0, ff_tiles, lambda n, carry, c=c: (twin_hidden(c, n).wait_send(), carry)[1], 0)
    for cond in (None, is_mid, is_end):
        sent = [copy for when, copy in unsent if when is cond]

        def drain(sent=sent):
            for copy in sent:
                copy().wait_send()

        if cond is None:
            drain()
        else:
            pl.when(cond)(drain)
    assert len(keys) <= SEMS, len(keys)


def fused_body(tokens, expert_ids, combine_weights, w_gate, w_up, w_down):
    experts = lax.axis_size("expert")
    toks, width = tokens.shape
    top = expert_ids.shape[1]
    cap = min(toks, 5 * toks * top // (4 * experts))
    share, ff = w_down.shape[2], w_gate.shape[2]
    half = share // 2
    expert_iota = lax.broadcasted_iota(jnp.int32, (1, experts, 1), 1)
    chosen = expert_ids.T[:, None, :] == expert_iota
    table = jnp.sum(jnp.where(chosen, combine_weights.T[:, None, :], 0.0), axis=0)
    anywhere = pl.BlockSpec(memory_space=pl.ANY)
    inside = pl.BlockSpec(memory_space=pltpu.VMEM)
    n = LAYERS
    buffers = [
        pltpu.VMEM((n, toks, share), BF16),
        pltpu.VMEM((n, 2, toks, half), BF16),
        pltpu.VMEM((n, 4, cap, half), BF16),
        pltpu.VMEM((n, 4, cap, width), BF16),
        pltpu.VMEM((n, 4 * cap, 2 * ff), BF16),
        pltpu.VMEM((n, 4, cap, share), BF16),
        pltpu.VMEM((4 * cap, 128), F32),
        pltpu.VMEM((n, 4, experts, toks), F32),
        pltpu.VMEM((n, 4, experts, toks), jnp.int32),
        pltpu.VMEM((n, 4, 2 * cap, toks), BF16),
        pltpu.VMEM((n, 2, 2, cap, half), BF16),
        pltpu.VMEM((n, 2, toks, half), BF16),
        pltpu.VMEM((n, 2, toks, half), BF16),
        pltpu.VMEM((n - 1, toks, share), BF16),
        pltpu.VMEM((n - 1, toks, share), BF16),
        pltpu.VMEM((2, toks, share), BF16),
        pltpu.VMEM(w_gate.shape[1:], BF16),
        pltpu.VMEM(w_up.shape[1:], BF16),
        pltpu.VMEM(w_down.shape[1:], BF16),
    ]
    return pl.pallas_call(
        functools.partial(moe_kernel, cap),
        out_shape=jax.ShapeDtypeStruct((toks, share), BF16),
        in_specs=[anywhere, inside, anywhere, anywhere, anywhere],
        out_specs=inside,
        scratch_shapes=buffers + [
            pltpu.SemaphoreType.DMA((SEMS,)), pltpu.SemaphoreType.DMA((SEMS,)), pltpu.SemaphoreType.DMA((4,)),
        ],
        compiler_params=pltpu.CompilerParams(
            collective_id=0, has_side_effects=True, vmem_limit_bytes=60 * 1024 * 1024
        ),
    )(tokens, table, w_gate, w_up, w_down)


def split_dots(mine, weights):
    place = lax.axis_index("pipe")
    other = lax.ppermute(mine, "pipe", [(0, 1), (1, 0)])
    share = mine.shape[1]
    totals = []
    for weight in weights:
        own = lax.dynamic_slice_in_dim(weight, place * share, share, 0)
        far = lax.dynamic_slice_in_dim(weight, (1 - place) * share, share, 0)
        total = jnp.dot(mine, own, preferred_element_type=jnp.float32)
        totals.append(total + jnp.dot(other, far, preferred_element_type=jnp.float32))
    return totals


def body(tokens, expert_ids, combine_weights, w_gate, w_up, w_down):
    experts = lax.axis_size("expert")
    tok_rows, model_width = tokens.shape
    top_count = expert_ids.shape[1]
    capacity = min(tok_rows, 5 * tok_rows * top_count // (4 * experts))
    slot_count = experts * capacity
    out_width = w_down.shape[2]
    expert_iota = lax.broadcasted_iota(jnp.int32, (1, 1, experts), 2)
    chosen = (expert_ids[:, :, None] == expert_iota).astype(jnp.int32)
    expert_hits = jnp.sum(chosen, axis=1)
    earlier = lax.broadcasted_iota(jnp.int32, (tok_rows, tok_rows), 1)
    earlier = earlier < lax.broadcasted_iota(jnp.int32, (tok_rows, tok_rows), 0)
    rank_table = jnp.dot(
        earlier.astype(jnp.bfloat16), expert_hits.astype(jnp.bfloat16), preferred_element_type=jnp.float32
    ).astype(jnp.int32)
    slot_rank = jnp.sum(chosen * rank_table[:, None, :], axis=2)
    target = expert_ids * capacity + slot_rank
    slot_iota = lax.broadcasted_iota(jnp.int32, (1, 1, slot_count), 2)
    slot_marks = target[:, :, None] == slot_iota
    placing = jnp.any(slot_marks, axis=1).astype(jnp.bfloat16)
    blend_table = jnp.sum(jnp.where(slot_marks, combine_weights[:, :, None], 0.0), axis=1)
    pipes = lax.axis_size("pipe")
    place = lax.axis_index("pipe")
    width_share = model_width // pipes
    tok_share = lax.dynamic_slice_in_dim(tokens, place * width_share, width_share, 1)
    packed = jnp.einsum("ts,td->sd", placing, tok_share, preferred_element_type=jnp.float32)
    packed = packed.astype(jnp.bfloat16).reshape(experts, capacity, width_share)
    received = lax.all_to_all(packed, "expert", split_axis=0, concat_axis=0, tiled=True)
    rows = received.reshape(slot_count, width_share)
    if pipes == 2:
        gate_acc, up_acc = split_dots(rows, [w_gate[0], w_up[0]])
    else:
        rows = lax.all_gather(rows, "pipe", axis=1, tiled=True)
        gate_acc = jnp.dot(rows, w_gate[0], preferred_element_type=jnp.float32)
        up_acc = jnp.dot(rows, w_up[0], preferred_element_type=jnp.float32)
    hidden_rows = (jax.nn.silu(gate_acc) * up_acc).astype(jnp.bfloat16)
    if pipes == 2:
        (outputs,) = split_dots(hidden_rows, [w_down[0]])
    else:
        outputs = jnp.dot(
            lax.all_gather(hidden_rows, "pipe", axis=1, tiled=True),
            w_down[0],
            preferred_element_type=jnp.float32,
        )
    outgoing = outputs.astype(jnp.bfloat16).reshape(experts, capacity, out_width)
    returned_rows = lax.all_to_all(outgoing, "expert", split_axis=0, concat_axis=0, tiled=True)
    mixture = jnp.dot(
        blend_table,
        returned_rows.reshape(slot_count, out_width).astype(jnp.float32),
        precision=lax.Precision.HIGHEST,
        preferred_element_type=jnp.float32,
    )
    return mixture.astype(jnp.bfloat16)


def solution(mesh):
    placed = (
        P("expert", None),
        P("expert", None),
        P("expert", None),
        P("expert", None, "pipe"),
        P("expert", None, "pipe"),
        P("expert", None, "pipe"),
    )
    tree = mesh.shape["pipe"] == SIDE and mesh.shape["expert"] == LAYERS * SIDE * SIDE
    return jax.shard_map(
        fused_body if tree else body, mesh=mesh, in_specs=placed, out_specs=P("expert", "pipe"), check_vma=False
    )
```

```python
import functools
import jax
import jax.numpy as jnp
from jax import lax
from jax.experimental import pallas as pl
from jax.experimental.pallas import tpu as pltpu
from jax.sharding import PartitionSpec as P

LAYERS, SIDE = 4, 2
MESH = pl.DeviceIdType.MESH
BF16, F32 = jnp.bfloat16, jnp.float32
TILE = 256
SEMS = 176
IN, OUT = 0, 1


ORDER = (
    (("d1", 0, 0), ("z0", 0), ("d1", 0, 1), ("d2", 0, 1), ("d2", 0, 0), ("z0", 1), ("d3", 0, 1),),
    (("d3", 0, 0), ("d1", 1, 0), ("r3", 0), ("d1", 1, 1), ("d4", 0), ("d2", 1, 1), ("r3", 1), ("d2", 1, 0),),
    (("gu", 0, 0, 1), ("d3", 1, 0), ("d3", 1, 1), ("d1", 2, 0), ("gu", 0, 1, 2), ("d1", 2, 1), ("d4", 1),),
    (("d2", 2, 1), ("d2", 2, 0), ("gu", 1, 0, 2), ("d3", 2, 1), ("d3", 2, 0), ("gu", 1, 2, 1), ("d1", 3, 0),),
    (("gu", 1, 3, 1), ("d1", 3, 1), ("d2", 3, 0), ("d2", 3, 1), ("d4", 2), ("dn", 1), ("gu", 2, 0, 1),),
    (("d3", 3, 0), ("d3", 3, 1), ("c1", 1, 0, 1), ("gu", 2, 1, 2), ("c1", 1, 1, 1), ("c1", 1, 1, 0),),
    (("gu", 2, 3, 1), ("d4", 3), ("dn", 2), ("c1", 2, 0, 1), ("c2", 1, 1), ("c1", 2, 1, 1), ("gu", 3, 0, 4),),
    (("c1", 2, 1, 0), ("c2", 2, 1), ("dn", 3), ("c1", 3, 1, 1), ("c1", 3, 0, 1), ("c3", 1, 1),),
    (("gu", 0, 3, 1), ("c1", 3, 1, 0), ("c3", 2, 1), ("c2", 3, 1), ("c2", 3, 0), ("dn", 0), ("c1", 3, 0, 0),),
    (("c1", 2, 0, 0), ("c1", 0, 1, 1), ("c1", 0, 0, 1), ("c1", 1, 0, 0), ("c1", 0, 0, 0), ("c3", 3, 1),),
    (("zm", 1, 1), ("c2", 2, 0), ("c3", 3, 0), ("zm", 2, 1), ("c2", 1, 0), ("c1", 0, 1, 0), ("c2", 0, 1),),
    (("c3", 2, 0), ("zm", 2, 0), ("zm", 3, 1), ("c3", 1, 0), ("zm", 1, 0), ("c2", 0, 0), ("zm", 3, 0),),
    (("c3", 0, 1), ("fin", 1), ("c3", 0, 0), ("fin", 0),),
)

def moe_kernel(
    cap, tok_hbm, ids_hbm, weights_hbm, wg_hbm, wu_hbm, wd_hbm, out_ref,
    full, first, leaf, rows, hidden, outs, row_weight, tabs, slots, marks,
    trim, sums_out, sums_in, zsend, zpass, zfin, ids, shares, wg, wu, wd,
    send_sem, recv_sem, local_sem,
):
    p = lax.axis_index("pipe")
    me = lax.axis_index("expert")
    z, y, x = me // 4, lax.rem(me // 2, 2), lax.rem(me, 2)
    toks, share = full.shape[1:]
    half = share // 2
    ff = wg.shape[1]
    base = pl.multiple_of(p * share, 128)
    mid = lax.rem((z + 1) // 2, 2)
    is_mid, is_end = mid == 1, mid == 0
    step = 1 - 2 * (z // 2)

    def chip(zz, yy, xx):
        return {"pipe": p, "expert": zz * 4 + yy * 2 + xx}

    xn, yn, dn = chip(z, y, 1 - x), chip(z, 1 - y, x), chip(z, 1 - y, 1 - x)
    inward = chip(z + step, y, x)
    outward = chip(z - step * mid, y, x)
    twin = {"pipe": 1 - p, "expert": me}
    layer = z * 4
    e_x, e_y = layer + y * 2 + 1 - x, layer + (1 - y) * 2 + x
    g_me, g_y, g_x, g_d = y * 2 + x, (1 - y) * 2 + x, y * 2 + 1 - x, (1 - y) * 2 + 1 - x

    keys = {}
    unsent = []

    def sem(*key):
        return keys.setdefault(key, len(keys))

    def make(skey, rkey, source, slot, device):
        source, slot = (ref() if callable(ref) else ref for ref in (source, slot))
        return pltpu.make_async_remote_copy(
            src_ref=source, dst_ref=slot, send_sem=send_sem.at[sem("s", *skey)],
            recv_sem=recv_sem.at[sem("s", *rkey)], device_id=device, device_id_type=MESH,
        )

    def send(skey, rkey, source, slot, device, when=None):
        make(skey, rkey, source, slot, device).start()
        unsent.append((when, functools.partial(make, skey, rkey, source, slot, device)))

    def arrived(rkey, slot):
        make(rkey, rkey, slot, slot, xn).wait_recv()

    def cols(h):
        return pl.ds(h * half, half)

    def wide_cols(h):
        return pl.ds(pl.multiple_of(base + h * half, 128), half)

    def load_tokens():
        return pltpu.make_async_copy(tok_hbm.at[:, pl.ds(base, share)], full.at[0], local_sem.at[3])

    weight_loads = [
        pltpu.make_async_copy(wg_hbm.at[0], wg, local_sem.at[0]),
        pltpu.make_async_copy(wu_hbm.at[0], wu, local_sem.at[1]),
        pltpu.make_async_copy(wd_hbm.at[0], wd, local_sem.at[2]),
    ]
    routing = [
        pltpu.make_async_copy(ids_hbm, ids, local_sem.at[4]),
        pltpu.make_async_copy(weights_hbm, shares, local_sem.at[5]),
    ]
    for copy in routing:
        copy.start()
    load_tokens().start()
    barrier = pltpu.get_barrier_semaphore()
    for device in (xn, yn, dn, twin, inward):
        pl.semaphore_signal(barrier, inc=1, device_id=device, device_id_type=MESH)

    @pl.when(is_mid)
    def _():
        pl.semaphore_signal(barrier, inc=1, device_id=outward, device_id_type=MESH)

    for copy in weight_loads:
        copy.start()
    for copy in routing:
        copy.wait()
    experts = tabs.shape[2]
    table = jnp.zeros((experts, toks), F32)
    for k in range(ids.shape[0]):
        hit = ids[pl.ds(k, 1), :] == lax.broadcasted_iota(jnp.int32, (experts, toks), 0)
        table = table + jnp.where(hit, shares[pl.ds(k, 1), :], 0.0)
    tabs[0, g_me] = table

    def earlier():
        a = lax.broadcasted_iota(jnp.int32, (toks, toks), 0)
        return jnp.where(a < lax.broadcasted_iota(jnp.int32, (toks, toks), 1), 1.0, 0.0).astype(BF16)

    def rank(c, g):
        table = tabs[c, g]
        named = table > 0.0
        order = jnp.dot(jnp.where(named, 1.0, 0.0).astype(BF16), earlier(), preferred_element_type=F32)
        slots[c, g] = jnp.where(named, order.astype(jnp.int32), -1)

    def picks(c, g, e):
        place = slots[c, g, pl.ds(e, 1), :]
        return place == lax.broadcasted_iota(jnp.int32, (cap, toks), 0)

    def mark(c, k, g, other):
        marks[c, k, pl.ds(0, cap)] = jnp.where(picks(c, g, me), 1.0, 0.0).astype(BF16)
        marks[c, k, pl.ds(cap, cap)] = jnp.where(picks(c, g, other), 1.0, 0.0).astype(BF16)

    rank(0, g_me)
    pl.semaphore_wait(barrier, 5 + mid)
    load_tokens().wait()

    def z_hop(name, c, target, device, h, when):
        send(
            (name, h), ("zf", target, h), lambda: full.at[c, :, cols(h)],
            lambda: full.at[target, :, cols(h)], device, when,
        )
        if h == 0:
            send(
                (name, "t"), ("zf", target, "t"), lambda: tabs.at[c, g_me],
                lambda: tabs.at[target, g_me], device, when,
            )

    def z0(h):
        @pl.when(is_mid)
        def _():
            z_hop("own", 0, 1, inward, h, is_mid)
            z_hop("own_out", 0, 1, outward, h, is_mid)

        @pl.when(is_end)
        def _():
            z_hop("own_end", 0, 3, inward, h, is_end)

    def z_wait(c, h):
        arrived(("zf", c, h), full.at[c, :, cols(h)])
        if h == 0:
            arrived(("zf", c, "t"), tabs.at[c, g_me])

    def r3(h):
        @pl.when(is_mid)
        def _():
            z_wait(3, h)
            z_hop("pass3", 3, 2, inward, h, is_mid)

    def share_table(c):
        for name, device in (("y", yn), ("x", xn), ("d", dn)):
            key = ("tab" + name, c)
            send(key, key, tabs.at[c, g_me], tabs.at[c, g_me], device)

    def d1(c, h):
        if c in (1, 2):
            z_wait(c, h)

            @pl.when(is_mid)
            def _():
                z_hop(f"pass{c}", c, c + 1, outward, h, is_mid)
        if c == 3:
            @pl.when(is_end)
            def _():
                z_wait(3, h)
        if h == 0:
            share_table(c)
        key = ("first", c, h)
        send(key, key, full.at[c, :, cols(h)], first.at[c, h], xn if h else yn)

    def pack(c, k, h, g, source, device):
        packed = jnp.dot(marks[c, k], source, preferred_element_type=F32).astype(BF16)
        rows[c, g, :, wide_cols(h)] = packed[:cap]
        leaf[c, k] = packed[cap:]
        key = ("leaf", c, k)
        send(key, key, leaf.at[c, k], rows.at[c, g, :, wide_cols(h)], device)

    ready = {(0, "me")}

    def ranked(c, name, g):
        if (c, name) not in ready:
            ready.add((c, name))
            if name != "me":
                arrived(("tab" + name, c), tabs.at[c, g])
            rank(c, g)

    def d2(c, h):
        ranked(c, "me", g_me)
        mark(c, h, g_me, e_y if h else e_x)
        pack(c, h, h, g_me, full[c, :, cols(h)], yn if h else xn)

    def d3(c, h):
        name, g = ("x", g_x) if h else ("y", g_y)
        ranked(c, name, g)
        mark(c, 2 + h, g, e_y if h else e_x)
        arrived(("first", c, h), first.at[c, h])
        pack(c, 2 + h, h, g, first[c, h], yn if h else xn)

    def d4(c):
        for k, g, h in ((0, g_x, 0), (1, g_y, 1), (2, g_d, 0), (3, g_d, 1)):
            arrived(("leaf", c, k), rows.at[c, g, :, wide_cols(h)])
        mine = rows.at[c, :, :, pl.ds(base, share)]
        send(("twin", c), ("twin", c), mine, mine, twin)

    def twin_hidden(c, n):
        tile = hidden.at[c, :, pl.ds(pl.multiple_of(p * ff + n * TILE, TILE), TILE)]
        at = sem("s", "hidden", c, 0) + n
        return pltpu.make_async_remote_copy(
            src_ref=tile, dst_ref=tile, send_sem=send_sem.at[at], recv_sem=recv_sem.at[at],
            device_id=twin, device_id_type=MESH,
        )

    ff_tiles = ff // TILE

    loaded = set()

    def weights(*which):
        for i in which:
            if i not in loaded:
                loaded.add(i)
                weight_loads[i].wait()

    def gu(c, first_tile, tiles):
        for n in range(ff_tiles):
            sem("s", "hidden", c, n)
        if first_tile == 0:
            arrived(("twin", c), rows.at[c, :, :, pl.ds(0, share)])
        weights(0, 1)

        def tile(n, carry):
            at = pl.ds(pl.multiple_of(n * TILE, TILE), TILE)
            mine = rows[c].reshape(4 * cap, 2 * share)
            gate = jnp.dot(mine, wg[:, at], preferred_element_type=F32)
            up = jnp.dot(mine, wu[:, at], preferred_element_type=F32)
            value = (gate / (1.0 + jnp.exp(-gate)) * up).astype(BF16)
            hidden[c, :, pl.ds(pl.multiple_of(p * ff + n * TILE, TILE), TILE)] = value
            twin_hidden(c, n).start()
            return carry

        lax.fori_loop(first_tile, first_tile + tiles, tile, 0)

    def dn_(c):
        ranked(c, "d", g_d)
        for g in range(4):
            weight = tabs[c, g, pl.ds(me, 1), :]
            column = jnp.sum(jnp.where(picks(c, g, me), weight, 0.0), axis=1, keepdims=True)
            row_weight[pl.ds(g * cap, cap)] = jnp.broadcast_to(column, (cap, 128))
        weights(2)

        def landed(n, carry):
            twin_hidden(c, n).wait_recv()
            return carry

        lax.fori_loop(0, ff_tiles, landed, 0)

        def tile(n, carry):
            at = pl.ds(pl.multiple_of(n * TILE, TILE), TILE)
            value = jnp.dot(hidden[c], wd[:, at], preferred_element_type=F32)
            scale = row_weight[...]
            value = value * jnp.concatenate([scale] * (TILE // 128), axis=1)
            outs[c, :, :, at] = value.astype(BF16).reshape(4, cap, TILE)
            return carry

        lax.fori_loop(0, share // TILE, tile, 0)

    def c1(c, h, j):
        g = g_d if j else (g_y if h else g_x)
        key = ("trim", c, h, j)
        send(key, key, outs.at[c, g, :, cols(h)], trim.at[c, h, j], yn if h else xn)

    def spread(c, k, g, h, j):
        arrived(("trim", c, h, j), trim.at[c, h, j])
        dims = (((0,), (0,)), ((), ()))
        one = lax.dot_general(marks[c, k, pl.ds(0, cap)], outs[c, g, :, cols(h)], dims, preferred_element_type=F32)
        return one + lax.dot_general(marks[c, k, pl.ds(cap, cap)], trim[c, h, j], dims, preferred_element_type=F32)

    def c2(c, h):
        sums_out[c, h] = spread(c, 2 + h, g_x if h else g_y, h, 1).astype(BF16)
        key = ("sums", c, h)
        send(key, key, sums_out.at[c, h], sums_in.at[c, h], xn if h else yn)

    def layer_sum(c, h):
        value = spread(c, h, g_me, h, 0)
        arrived(("sums", c, h), sums_in.at[c, h])
        return value + sums_in[c, h].astype(F32)

    def z_sum(name, c, h, target, device, when):
        buffer, at = target
        send(
            (name, c, h), ("zpass" if buffer is zpass else "zfin", at, h),
            lambda: zsend.at[c - 1, :, cols(h)], lambda: buffer.at[at, :, cols(h)], device, when,
        )

    own = {}

    def c3(c, h):
        value = layer_sum(c, h)
        if c == 0:
            own[h] = value
            return
        zsend[c - 1, :, cols(h)] = value.astype(BF16)

        @pl.when(is_end)
        def _():
            z_sum("zend", c, h, (zfin, OUT) if c == 1 else (zpass, c - 2), inward, is_end)

    def zm(c, h):
        @pl.when(is_mid)
        def _():
            arrived(("zpass", c - 1, h), zpass.at[c - 1, :, cols(h)])
            total = zsend[c - 1, :, cols(h)].astype(F32) + zpass[c - 1, :, cols(h)].astype(F32)
            zsend[c - 1, :, cols(h)] = total.astype(BF16)
            z_sum("zmid", c, h, (zpass, 2) if c == 2 else (zfin, IN), outward if c == 3 else inward, is_mid)

    def fin(h):
        arrived(("zfin", IN, h), zfin.at[IN, :, cols(h)])

        @pl.when(is_mid)
        def _():
            arrived(("zfin", OUT, h), zfin.at[OUT, :, cols(h)])
            value = own[h] + zfin[IN, :, cols(h)].astype(F32) + zfin[OUT, :, cols(h)].astype(F32)
            out_ref[:, cols(h)] = value.astype(BF16)

        @pl.when(is_end)
        def _():
            out_ref[:, cols(h)] = (own[h] + zfin[IN, :, cols(h)].astype(F32)).astype(BF16)

    step_of = {
        "z0": z0, "r3": r3, "d1": d1, "d2": d2, "d3": d3, "d4": d4, "gu": gu, "dn": dn_,
        "c1": c1, "c2": c2, "c3": c3, "zm": zm, "fin": fin,
    }
    for entry in ORDER:
        for name, *numbers in entry:
            step_of[name](*numbers)
    for c in range(4):
        for n in range(ff_tiles):
            sem("s", "hidden", c, n)

    for c in range(4):
        lax.fori_loop(0, ff_tiles, lambda n, carry, c=c: (twin_hidden(c, n).wait_send(), carry)[1], 0)
    for cond in (None, is_mid, is_end):
        sent = [copy for when, copy in unsent if when is cond]

        def drain(sent=sent):
            for copy in sent:
                copy().wait_send()

        if cond is None:
            drain()
        else:
            pl.when(cond)(drain)
    assert len(keys) <= SEMS, len(keys)


def fused_body(tokens, expert_ids, combine_weights, w_gate, w_up, w_down):
    experts = lax.axis_size("expert")
    toks, width = tokens.shape
    top = expert_ids.shape[1]
    cap = min(toks, 5 * toks * top // (4 * experts))
    share, ff = w_down.shape[2], w_gate.shape[2]
    half = share // 2
    anywhere = pl.BlockSpec(memory_space=pl.ANY)
    inside = pl.BlockSpec(memory_space=pltpu.VMEM)
    n = LAYERS
    buffers = [
        pltpu.VMEM((n, toks, share), BF16),
        pltpu.VMEM((n, 2, toks, half), BF16),
        pltpu.VMEM((n, 4, cap, half), BF16),
        pltpu.VMEM((n, 4, cap, width), BF16),
        pltpu.VMEM((n, 4 * cap, 2 * ff), BF16),
        pltpu.VMEM((n, 4, cap, share), BF16),
        pltpu.VMEM((4 * cap, 128), F32),
        pltpu.VMEM((n, 4, experts, toks), F32),
        pltpu.VMEM((n, 4, experts, toks), jnp.int32),
        pltpu.VMEM((n, 4, 2 * cap, toks), BF16),
        pltpu.VMEM((n, 2, 2, cap, half), BF16),
        pltpu.VMEM((n, 2, toks, half), BF16),
        pltpu.VMEM((n, 2, toks, half), BF16),
        pltpu.VMEM((n - 1, toks, share), BF16),
        pltpu.VMEM((n - 1, toks, share), BF16),
        pltpu.VMEM((2, toks, share), BF16),
        pltpu.VMEM((top, toks), jnp.int32),
        pltpu.VMEM((top, toks), F32),
        pltpu.VMEM(w_gate.shape[1:], BF16),
        pltpu.VMEM(w_up.shape[1:], BF16),
        pltpu.VMEM(w_down.shape[1:], BF16),
    ]
    return pl.pallas_call(
        functools.partial(moe_kernel, cap),
        out_shape=jax.ShapeDtypeStruct((toks, share), BF16),
        in_specs=[anywhere] * 6,
        out_specs=inside,
        scratch_shapes=buffers + [
            pltpu.SemaphoreType.DMA((SEMS,)), pltpu.SemaphoreType.DMA((SEMS,)), pltpu.SemaphoreType.DMA((6,)),
        ],
        compiler_params=pltpu.CompilerParams(
            collective_id=0, has_side_effects=True, vmem_limit_bytes=60 * 1024 * 1024
        ),
    )(tokens, expert_ids.T, combine_weights.T, w_gate, w_up, w_down)


def split_dots(mine, weights):
    place = lax.axis_index("pipe")
    other = lax.ppermute(mine, "pipe", [(0, 1), (1, 0)])
    share = mine.shape[1]
    totals = []
    for weight in weights:
        own = lax.dynamic_slice_in_dim(weight, place * share, share, 0)
        far = lax.dynamic_slice_in_dim(weight, (1 - place) * share, share, 0)
        total = jnp.dot(mine, own, preferred_element_type=jnp.float32)
        totals.append(total + jnp.dot(other, far, preferred_element_type=jnp.float32))
    return totals


def body(tokens, expert_ids, combine_weights, w_gate, w_up, w_down):
    experts = lax.axis_size("expert")
    tok_rows, model_width = tokens.shape
    top_count = expert_ids.shape[1]
    capacity = min(tok_rows, 5 * tok_rows * top_count // (4 * experts))
    slot_count = experts * capacity
    out_width = w_down.shape[2]
    expert_iota = lax.broadcasted_iota(jnp.int32, (1, 1, experts), 2)
    chosen = (expert_ids[:, :, None] == expert_iota).astype(jnp.int32)
    expert_hits = jnp.sum(chosen, axis=1)
    earlier = lax.broadcasted_iota(jnp.int32, (tok_rows, tok_rows), 1)
    earlier = earlier < lax.broadcasted_iota(jnp.int32, (tok_rows, tok_rows), 0)
    rank_table = jnp.dot(
        earlier.astype(jnp.bfloat16), expert_hits.astype(jnp.bfloat16), preferred_element_type=jnp.float32
    ).astype(jnp.int32)
    slot_rank = jnp.sum(chosen * rank_table[:, None, :], axis=2)
    target = expert_ids * capacity + slot_rank
    slot_iota = lax.broadcasted_iota(jnp.int32, (1, 1, slot_count), 2)
    slot_marks = target[:, :, None] == slot_iota
    placing = jnp.any(slot_marks, axis=1).astype(jnp.bfloat16)
    blend_table = jnp.sum(jnp.where(slot_marks, combine_weights[:, :, None], 0.0), axis=1)
    pipes = lax.axis_size("pipe")
    place = lax.axis_index("pipe")
    width_share = model_width // pipes
    tok_share = lax.dynamic_slice_in_dim(tokens, place * width_share, width_share, 1)
    packed = jnp.einsum("ts,td->sd", placing, tok_share, preferred_element_type=jnp.float32)
    packed = packed.astype(jnp.bfloat16).reshape(experts, capacity, width_share)
    received = lax.all_to_all(packed, "expert", split_axis=0, concat_axis=0, tiled=True)
    rows = received.reshape(slot_count, width_share)
    if pipes == 2:
        gate_acc, up_acc = split_dots(rows, [w_gate[0], w_up[0]])
    else:
        rows = lax.all_gather(rows, "pipe", axis=1, tiled=True)
        gate_acc = jnp.dot(rows, w_gate[0], preferred_element_type=jnp.float32)
        up_acc = jnp.dot(rows, w_up[0], preferred_element_type=jnp.float32)
    hidden_rows = (jax.nn.silu(gate_acc) * up_acc).astype(jnp.bfloat16)
    if pipes == 2:
        (outputs,) = split_dots(hidden_rows, [w_down[0]])
    else:
        outputs = jnp.dot(
            lax.all_gather(hidden_rows, "pipe", axis=1, tiled=True),
            w_down[0],
            preferred_element_type=jnp.float32,
        )
    outgoing = outputs.astype(jnp.bfloat16).reshape(experts, capacity, out_width)
    returned_rows = lax.all_to_all(outgoing, "expert", split_axis=0, concat_axis=0, tiled=True)
    mixture = jnp.dot(
        blend_table,
        returned_rows.reshape(slot_count, out_width).astype(jnp.float32),
        precision=lax.Precision.HIGHEST,
        preferred_element_type=jnp.float32,
    )
    return mixture.astype(jnp.bfloat16)


def solution(mesh):
    placed = (
        P("expert", None),
        P("expert", None),
        P("expert", None),
        P("expert", None, "pipe"),
        P("expert", None, "pipe"),
        P("expert", None, "pipe"),
    )
    tree = mesh.shape["pipe"] == SIDE and mesh.shape["expert"] == LAYERS * SIDE * SIDE
    return jax.shard_map(
        fused_body if tree else body, mesh=mesh, in_specs=placed, out_specs=P("expert", "pipe"), check_vma=False
    )
```
